32 devices in a mesh: field: 2 (over x), tile: 16 (over z, y, core).
Axes of the slice: x: 2, y: 2, z: 4, core: 2. Of those that a mesh axis runs over, the one named last changes fastest.
Arguments:
- psi_det: float32 [128, 8, 8, 128], P(('field', 'tile')), parts along dimension 0, may hold values from -6 to 6
- phi_det: float32 [128, 8, 8, 128], P(('field', 'tile')), parts along dimension 0, may hold values from 0.25 to 4
- dest_tile: int32 [128, 8, 1], P(('field', 'tile')), parts along dimension 0, may hold values from 0 to 15; in each aligned block of 32 rows (0 to 31, 32 to 63, ..., all dimensions but the last counted through in order) at most 4 rows name the same one
- dest_cell: int32 [128, 8], P(('field', 'tile')), parts along dimension 0, may hold values from 0 to 3
- kernel_id: int32 [128, 8], P(('field', 'tile')), parts along dimension 0, may hold values from 0 to 7
- intersection_weight: float32 [128, 8], P(('field', 'tile')), parts along dimension 0, may hold values from 0.5 to 1.5
- kernels: float32 [8, 128, 128], replicated, may hold values from 0 to 2
- row_offsets: int32 [16, 16], P('field'), parts along dimension 0, may hold values from -8 to 8
- col_offsets: int32 [16, 16], P('field'), parts along dimension 0, may hold values from -64 to 64
Outputs:
- best: float32 [256, 512], P(('field', 'tile')), parts along dimension 0
The draws below stay inside these ranges and needn't reach their ends.
There are 2 independent parts, one for each index of `field`. The reference program is written for one: setup_inputs(seed, part) draws one part's arguments, and reference() takes and returns one part's arrays. A program takes and returns all parts, laid end to end along the dimension named above; an argument that names none is the same for every part. Nothing has to cross between parts.
Inputs may be any that keep to these rules, and one draw needn't show every extreme that they name: `dest_tile`: among one device's 4 blocks over all 8 epochs no tile is named more than 4 times, a bound that some block reaches. `kernels`: every kernel is tridiagonal; kernels[k, i, j] = 0 whenever |i - j| > 1.
All inputs are finite; a program needn't handle non-finite values.
Results may differ from the reference program's by a relative error of at most 0.0003.
Values sent between devices are 32-bit elements; how exact they have to be, the bound alone decides.
A program may use at most 64 MiB of HBM per device.

```python
import math
import jax
import jax.numpy as jnp
import numpy as np
from jax import lax

ROWS = 8
CELLS = 4
BLOCKW = 128
EPOCHS = 8
VELS = 16
KERNELS = 8
XREACH = 64
RREACH = 8
CAP = 4
BLOCKS = 64
N_TILE = 16


def draw_kernels(key, part):
    key_main = jax.random.fold_in(key, 101)
    key_upper = jax.random.fold_in(key, 202)
    key_lower = jax.random.fold_in(key, 303)
    main = jax.random.uniform(key_main, (KERNELS, BLOCKW), jnp.float32, 1.0, 2.0)
    upper = jax.random.uniform(key_upper, (KERNELS, BLOCKW), jnp.float32, 0.1, 0.5)
    lower = jax.random.uniform(key_lower, (KERNELS, BLOCKW), jnp.float32, 0.1, 0.5)
    positions = jnp.arange(BLOCKW)
    diagonal_mask = (positions[:, None] == positions[None, :]).astype(jnp.float32)
    upper_mask = (positions[None, :] == positions[:, None] + 1).astype(jnp.float32)
    lower_mask = (positions[None, :] == positions[:, None] - 1).astype(jnp.float32)
    return main[:, :, None] * diagonal_mask + upper[:, :, None] * upper_mask + lower[:, :, None] * lower_mask


def set_ends(values, stream_key, least, high):
    place = [jax.random.randint(jax.random.fold_in(stream_key, axis), (), 0, length) for axis, length in enumerate(values.shape)]
    main_axis = values.shape.index(max(values.shape))
    beside = place[:main_axis] + [(place[main_axis] + 1) % values.shape[main_axis]] + place[main_axis + 1:]
    return values.at[tuple(place)].set(least).at[tuple(beside)].set(high)


def level_of(key, extent, cuts, least, high):
    def one(position, blocks):
        draws = jax.random.uniform(jax.random.fold_in(jax.random.fold_in(key, 6), position), (blocks,), jnp.float32, least / len(cuts), high / len(cuts))
        return jnp.repeat(jnp.exp(draws), extent[position] // blocks).reshape((-1,) + (1,) * (len(extent) - position - 1))

    factor_of = one(*cuts[0])
    for cut in cuts[1:]:
        factor_of = factor_of * one(*cut)
    return factor_of


def deal_out(rng, own, number, rows, number_of, top, most, skew):
    ranking = jax.random.permutation(rng, number_of)
    packed, ordinary = shares(number_of, rows * top, most, skew, True), shares(number_of, rows * top, most, skew, False)
    places = jnp.arange(number_of)

    def named(tallies, turn):
        used = int((tallies > 0).sum())
        fixed = max(1, used // 4)
        passed = fixed + (places - fixed + turn * (used - fixed)) % max(1, number_of - fixed)
        return jnp.zeros((number_of,), jnp.int32).at[ranking[jnp.where(places < fixed, places, passed)]].set(jnp.asarray(tallies, jnp.int32))

    tallies = jnp.where(number % 4 == 0, named(packed, number // 4), named(ordinary, number - number // 4 - 1))
    mixed = jax.random.permutation(jax.random.fold_in(own, 3), number_of)
    donor, receiver = mixed[0:number_of // 2 * 2:2], mixed[1:number_of // 2 * 2:2]
    room = jnp.minimum(tallies[donor] - 1, most - tallies[receiver]) // 2
    room = jnp.where((donor == ranking[0]) | (receiver == ranking[0]) | (tallies[receiver] == 0), 0, jnp.maximum(room, 0))
    passed = jax.random.randint(jax.random.fold_in(own, 4), (number_of // 2,), 0, 1 << 20) % (room + 1)
    tallies = tallies.at[donor].add(-passed).at[receiver].add(passed)
    labels = jnp.searchsorted(jnp.cumsum(tallies), jnp.arange(rows * top), side="right").astype(jnp.int32)
    table = labels.reshape(top, rows).T
    table = table[jax.random.permutation(jax.random.fold_in(own, 1), rows)]
    turn = jax.random.randint(jax.random.fold_in(own, 2), (rows, 1), 0, top)
    return jnp.take_along_axis(table, (jnp.arange(top)[None, :] + turn) % top, axis=1)


def shares(count, total, limit, skew, full):
    loads = [(1 << 20) // math.isqrt(rank ** skew) + 1 for rank in range(1, count + 1)]
    largest = limit if full else min(limit, max(-(-total // count), total * loads[0] // sum(loads)))
    least = 1 if total - largest >= count - 1 else 0
    counts, rest = [largest] + [least] * (count - 1), total - largest - least * (count - 1)
    while rest > 0:
        free = [i for i in range(1, count) if counts[i] < largest] or [i for i in range(1, count) if counts[i] < limit]
        pool, left = sum([loads[i] for i in free]), rest
        for i in free:
            more = min(limit - counts[i], max(1, left * loads[i] // pool), rest)
            counts[i] = counts[i] + more
            rest = rest - more
    return np.array(counts)


def bell_draw(rng, extent, spread, most, cuts=(), kind=jnp.bfloat16):
    array = spread * jax.random.normal(rng, extent, jnp.float32)
    if cuts:
        array = array * level_of(rng, extent, cuts, -0.22, 0.18)
    return jnp.clip(array, -most, most).astype(kind)


def setup_inputs(seed: int = 0, part: int = 0) -> dict:
    splits = jax.random.split(jax.random.key(seed), 10)
    own_keys = jax.random.split(jax.random.fold_in(splits[9], part), 10)
    psi_det = bell_draw(own_keys[0], (BLOCKS, EPOCHS, ROWS, BLOCKW), 1.0, 6.0, ((0, 16),), jnp.float32)
    phi_det = jnp.clip(jnp.exp(math.log(4.0) - 2.7725887 * jax.random.uniform(own_keys[1], (BLOCKS, EPOCHS, ROWS, BLOCKW), jnp.float32) ** level_of(own_keys[1], (BLOCKS, EPOCHS, ROWS, BLOCKW), ((0, 16),), -0.2, 0.2)), 0.25, 4.0)
    dest_tile_keys = jax.random.split(jax.random.fold_in(own_keys[2], 1), BLOCKS * EPOCHS // (CELLS * EPOCHS))
    dest_tile_turns = jax.random.permutation(jax.random.fold_in(own_keys[2], 3), BLOCKS * EPOCHS // (CELLS * EPOCHS))
    dest_tile = jax.vmap(lambda own, number: deal_out(jax.random.fold_in(own_keys[2], 2), own, number, CELLS * EPOCHS, N_TILE, 1, CAP, 2))(dest_tile_keys, dest_tile_turns).reshape((BLOCKS, EPOCHS, 1))
    dest_cell = set_ends(jax.random.randint(own_keys[3], (BLOCKS, EPOCHS), 0, CELLS), jax.random.fold_in(own_keys[3], 1), 0, CELLS - 1).astype(jnp.int32)
    kernel_id = set_ends(jax.random.randint(own_keys[4], (BLOCKS, EPOCHS), 0, KERNELS), jax.random.fold_in(own_keys[4], 1), 0, KERNELS - 1).astype(jnp.int32)
    intersection_weight = jnp.clip(0.5 + 1.0 * jax.random.uniform(own_keys[5], (BLOCKS, EPOCHS), jnp.float32) ** level_of(own_keys[5], (BLOCKS, EPOCHS), ((0, 16),), -0.2, 0.2), 0.5, 1.5)
    kernels = draw_kernels(jax.random.fold_in(splits[9], 71), part)
    row_offsets = set_ends(jax.random.randint(own_keys[7], (EPOCHS, VELS), 0 - RREACH, RREACH + 1), jax.random.fold_in(own_keys[7], 1), 0 - RREACH, RREACH).astype(jnp.int32)
    col_offsets = set_ends(jax.random.randint(own_keys[8], (EPOCHS, VELS), 0 - XREACH, XREACH + 1), jax.random.fold_in(own_keys[8], 1), 0 - XREACH, XREACH).astype(jnp.int32)
    return {"psi_det": psi_det, "phi_det": phi_det, "dest_tile": dest_tile, "dest_cell": dest_cell, "kernel_id": kernel_id, "intersection_weight": intersection_weight, "kernels": kernels, "row_offsets": row_offsets, "col_offsets": col_offsets}


def reproject(payload, kernel_ids, weights, kernels_table):
    row_total = payload.shape[0]
    group_size = math.gcd(row_total, 32)

    def one_group(group_items):
        pieces, chosen_ids, factors = group_items
        chosen = kernels_table[chosen_ids]
        moved = jnp.einsum('ncrb,nbk->ncrk', pieces, chosen, precision=lax.Precision.HIGHEST)
        return moved * factors[:, None, None, None]
    grouped = (payload.reshape((row_total // group_size, group_size) + payload.shape[1:]), kernel_ids.reshape(row_total // group_size, group_size), weights.reshape(row_total // group_size, group_size))
    return lax.map(one_group, grouped).reshape(payload.shape)

def reference(psi_det, phi_det, dest_tile, dest_cell, kernel_id, intersection_weight, kernels, row_offsets, col_offsets):
    block_count = psi_det.shape[0]
    row_total = block_count * EPOCHS
    blocks = jnp.stack([psi_det, phi_det], axis=2).reshape(row_total, 2, ROWS, BLOCKW)
    moved = reproject(blocks, kernel_id.reshape(row_total).astype(jnp.int32), intersection_weight.reshape(row_total), kernels)
    epoch_of = jnp.arange(row_total, dtype=jnp.int32) % EPOCHS
    target = (dest_tile.reshape(row_total).astype(jnp.int32) * EPOCHS + epoch_of) * CELLS + dest_cell.reshape(row_total).astype(jnp.int32)
    summed = jax.ops.segment_sum(moved.reshape(row_total, -1), target, num_segments=N_TILE * EPOCHS * CELLS)
    sky_image = summed.reshape(N_TILE, EPOCHS, CELLS, 2, ROWS, BLOCKW).transpose(3, 1, 0, 4, 2, 5)
    total_rows = N_TILE * ROWS
    side_cols = CELLS * BLOCKW
    sky_image = sky_image.reshape(2, EPOCHS, total_rows, side_cols)
    padded = jnp.pad(sky_image, ((0, 0), (0, 0), (RREACH, RREACH), (XREACH, XREACH)))

    def one_velocity(highest, offsets):
        row_shift, col_shift = offsets
        sums = jnp.zeros((2, total_rows, side_cols), jnp.float32)
        for epoch_idx in range(EPOCHS):
            start_row = (RREACH + row_shift[epoch_idx]).astype(jnp.int32)
            start_col = (XREACH + col_shift[epoch_idx]).astype(jnp.int32)
            sums = sums + lax.dynamic_slice(padded[:, epoch_idx], (jnp.int32(0), start_row, start_col), (2, total_rows, side_cols))
        score = sums[0] / jnp.sqrt(jnp.maximum(sums[1], 1.0))
        return (jnp.maximum(highest, score), None)
    start = jnp.full((total_rows, side_cols), -jnp.inf, jnp.float32)
    result = lax.scan(one_velocity, start, (row_offsets.T, col_offsets.T))
    return result[0]
```

```python
import functools

import jax
import jax.numpy as jnp
from jax import lax
from jax.experimental import pallas as pl
from jax.experimental.pallas import tpu as pltpu
from jax.sharding import PartitionSpec as P

MESH = pl.DeviceIdType.MESH
LANES = 128
UNROLL = 4


def split2(x):
    hi = x.astype(jnp.bfloat16)
    return hi, (x - hi.astype(jnp.float32)).astype(jnp.bfloat16)


def select_dot(onehot2, x):
    return jnp.dot(
        onehot2, jnp.concatenate(split2(x), axis=0), preferred_element_type=jnp.float32
    )


def kernel(
    dims,
    psi_hbm,
    phi_hbm,
    tile_hbm,
    cell_hbm,
    kid_hbm,
    weight_hbm,
    kern_hbm,
    row_hbm,
    col_hbm,
    out_ref,
    psi_ref,
    phi_ref,
    tile_ref,
    cell_ref,
    kid_ref,
    weight_ref,
    kern_ref,
    row_ref,
    col_ref,
    psi_sums,
    taps,
    moved,
    send,
    recv,
    codes_out,
    codes_in,
    own,
    low,
    high,
    field,
    in_sem,
    send_sem,
    recv_sem,
    code_send_sem,
    code_recv_sem,
    halo_send_sem,
    halo_recv_sem,
    near_sem,
):
    n, cap, cells, epochs, rows, kernels, vels = dims
    items = cells * epochs
    slots = n * cap
    pitch = 2 * rows
    parts = (rows, rows)
    firsts = (0, rows)
    chunks = len(parts)
    targets = cells * epochs
    code_lanes = codes_in.shape[2]
    me = lax.axis_index("tile")
    half = n // 2
    side = me // half

    def across(act):
        def step_of(step, carry):
            act((1 - side) * half + lax.rem(me + step, half))
            return carry

        lax.fori_loop(0, half, step_of, 0, unroll=8)

    def beside(act):
        def step_of(step, carry):
            act(side * half + lax.rem(me + step, half))
            return carry

        lax.fori_loop(1, half, step_of, 0, unroll=7)

    def around(act):
        def step_of(step, carry):
            act(lax.rem(me + step, n))
            return carry

        lax.fori_loop(1, n, step_of, 0, unroll=5)

    barrier = pltpu.get_barrier_semaphore()
    around(
        lambda peer: pl.semaphore_signal(
            barrier, inc=1, device_id={"tile": peer}, device_id_type=MESH
        )
    )

    sources = (tile_hbm, cell_hbm, kid_hbm, weight_hbm, kern_hbm, psi_hbm, phi_hbm, row_hbm, col_hbm)
    places = (tile_ref, cell_ref, kid_ref, weight_ref, kern_ref, psi_ref, phi_ref, row_ref, col_ref)
    loads = [
        pltpu.make_async_copy(source, place, in_sem.at[i])
        for i, (source, place) in enumerate(zip(sources, places))
    ]
    for load in loads:
        load.start()
    field[...] = jnp.zeros_like(field)

    lane = lax.broadcasted_iota(jnp.int32, (8, LANES), 1)
    sub = lax.broadcasted_iota(jnp.int32, (8, LANES), 0)
    loads[4].wait()
    for k in range(kernels):
        sums = [jnp.zeros((8, LANES), jnp.float32)] * 3
        for group in range(LANES // 8):
            rows_of = kern_ref[k, pl.ds(group * 8, 8), :]
            gap = lane - sub - group * 8
            sums = [
                jnp.where(gap == off, rows_of, total) for off, total in zip((1, 0, -1), sums)
            ]
        for tap in range(3):
            taps[pl.ds(tap * kernels + k, 1), :] = jnp.sum(sums[tap], axis=0, keepdims=True)

    for load in loads[:4]:
        load.wait()
    row_tile = jnp.full((8, LANES), -1, jnp.int32)
    row_code = jnp.zeros((8, LANES), jnp.int32)
    col_tile = [jnp.full((8, LANES), -1, jnp.int32) for _ in range(items // 8)]
    for b in range(cells):
        for e in range(epochs):
            i = b * epochs + e
            tile = tile_ref[b, e]
            row_tile = jnp.where(lane == i, tile, row_tile)
            row_code = jnp.where(lane == i, cell_ref[b, e] * epochs + e + 1, row_code)
            col_tile[i // 8] = jnp.where(sub == i % 8, tile, col_tile[i // 8])

    def move(k, ref):
        for b in range(cells):
            for e in range(epochs):
                i = b * epochs + e
                kid = kid_ref[b, e]
                weight = weight_ref[b, e]
                before = taps[pl.ds(kid, 1), :] * weight
                centre = taps[pl.ds(kernels + kid, 1), :] * weight
                after = taps[pl.ds(2 * kernels + kid, 1), :] * weight
                x = ref[b, e]
                moved[pl.ds(i * pitch + k * rows, rows), :] = (
                    pltpu.roll(x, 1, 1) * before
                    + x * centre
                    + pltpu.roll(x, LANES - 1, 1) * after
                )

    col_tile = jnp.concatenate(col_tile, axis=0)
    item_lane = lax.broadcasted_iota(jnp.int32, (items, LANES), 1)
    item_sub = lax.broadcasted_iota(jnp.int32, (items, LANES), 0)
    same = (col_tile == row_tile[0:1, :]).astype(jnp.float32)
    row_rank = jnp.sum(jnp.where(item_sub < item_lane, same, 0.0), axis=0, keepdims=True)
    col_rank = jnp.sum(jnp.where(item_lane < item_sub, same, 0.0), axis=1, keepdims=True)
    row_place = jnp.where(
        row_tile[0:1, :] >= 0, row_tile[0:1, :] * cap + row_rank.astype(jnp.int32), -1
    )
    pick = (
        lax.broadcasted_iota(jnp.int32, (slots, LANES), 0) == row_place
    ).astype(jnp.float32)[:, :items]
    pick2 = jnp.concatenate([pick] * 2, axis=1).astype(jnp.bfloat16)

    def block(c, t):
        span = cap * parts[c]
        return pl.ds(pl.multiple_of(slots * firsts[c] + t * span, span), span)

    def pack(c):
        for q in range(0, parts[c], 2):
            x = jnp.concatenate(
                [
                    moved[pl.ds(firsts[c] + q + h, items, stride=pitch), :]
                    for h in range(2)
                ],
                axis=1,
            )
            packed = select_dot(pick2, x)
            for h in range(2):
                send[pl.ds(slots * firsts[c] + q + h, slots, stride=parts[c]), :] = packed[
                    :, h * LANES : (h + 1) * LANES
                ]
        recv[block(c, me), :] = send[block(c, me), :]

    loads[5].wait()
    move(0, psi_ref)
    pack(0)
    named = jnp.where(
        lax.broadcasted_iota(jnp.int32, (n, LANES), 0) == row_tile[0:1, :],
        row_code[0:1, :].astype(jnp.float32),
        0.0,
    )[:, :items].astype(jnp.bfloat16)
    spread = (
        lax.broadcasted_iota(jnp.int32, (items, code_lanes), 1)
        == me * cap + col_rank.astype(jnp.int32)
    ).astype(jnp.bfloat16)
    codes = jnp.dot(named, spread, preferred_element_type=jnp.float32)
    for t in range(n):
        codes_out[t] = codes[t : t + 1, :]

    codes_in[me] = codes_out[me]

    def code_copy(peer):
        return pltpu.make_async_remote_copy(
            src_ref=codes_out.at[peer],
            dst_ref=codes_in.at[me],
            send_sem=code_send_sem,
            recv_sem=code_recv_sem,
            device_id={"tile": peer},
            device_id_type=MESH,
        )

    def all_codes():
        return pltpu.make_async_remote_copy(
            src_ref=codes_out.at[pl.ds(0, n - 1)],
            dst_ref=codes_in.at[pl.ds(0, n - 1)],
            send_sem=code_send_sem,
            recv_sem=code_recv_sem,
            device_id={"tile": lax.rem(me + 1, n)},
            device_id_type=MESH,
        )

    def data_copy(c, peer):
        return pltpu.make_async_remote_copy(
            src_ref=send.at[block(c, peer)],
            dst_ref=recv.at[block(c, me)],
            send_sem=send_sem.at[c],
            recv_sem=recv_sem.at[c],
            device_id={"tile": peer},
            device_id_type=MESH,
        )

    def all_data(c):
        rest = pl.ds(slots * firsts[c], (n - 1) * cap * parts[c])
        return pltpu.make_async_remote_copy(
            src_ref=send.at[rest],
            dst_ref=recv.at[rest],
            send_sem=send_sem.at[c],
            recv_sem=recv_sem.at[c],
            device_id={"tile": lax.rem(me + 1, n)},
            device_id_type=MESH,
        )

    def start_codes(peer):
        code_copy(peer).start()

    def start_data(c):
        return lambda peer: data_copy(c, peer).start()

    pl.semaphore_wait(barrier, n - 1)
    around(start_codes)
    around(start_data(0))
    loads[6].wait()
    move(1, phi_ref)
    for c in range(1, chunks):
        pack(c)
        around(start_data(c))
    for load in loads[7:]:
        load.wait()

    all_codes().wait_recv()
    code_row = codes_in[0]
    for t in range(1, n):
        code_row = code_row + codes_in[t]
    land = (
        lax.broadcasted_iota(jnp.int32, (targets, code_lanes), 0) + 1
        == code_row.astype(jnp.int32)
    ).astype(jnp.float32)[:, :slots]
    land2 = jnp.concatenate([land] * 2, axis=1).astype(jnp.bfloat16)

    def share(c):
        return pl.ds(targets * firsts[c], targets * parts[c])

    def halo(c, way):
        peer = (lax.rem(me + 1, n), lax.rem(me + n - 1, n))[way]
        return pltpu.make_async_remote_copy(
            src_ref=own.at[share(c)],
            dst_ref=(low, high)[way].at[share(c)],
            send_sem=halo_send_sem.at[way, c],
            recv_sem=halo_recv_sem.at[way, c],
            device_id={"tile": peer},
            device_id_type=MESH,
        )

    def start_halo(c):
        @pl.when(me < n - 1)
        def _():
            halo(c, 0).start()

        @pl.when(me > 0)
        def _():
            halo(c, 1).start()

    def row_at(k, target):
        return ((k * (cells + 2) + 1) * epochs + target) * 3 * rows

    def sum_chunk(c):
        part = parts[c]
        for q in range(0, part, 2):
            x = jnp.concatenate(
                [
                    recv[pl.ds(slots * firsts[c] + q + h, slots, stride=part), :]
                    for h in range(2)
                ],
                axis=1,
            )
            summed = select_dot(land2, x)
            for h in range(2):
                k, r = divmod(firsts[c] + q + h, rows)
                piece = summed[:, h * LANES : (h + 1) * LANES]
                own[pl.ds(targets * firsts[c] + q + h, targets, stride=part), :] = piece
                field[pl.ds(row_at(k, 0) + rows + r, targets, stride=3 * rows), :] = piece

    def place(ref, c, offset):
        part = parts[c]
        k, r = divmod(firsts[c], rows)
        for target in range(targets):
            field[pl.ds(row_at(k, target) + offset + r, part), :] = ref[
                pl.ds(targets * firsts[c] + target * part, part), :
            ]

    def finish_halo(c):
        @pl.when(me > 0)
        def _():
            halo(c, 0).wait_recv()
            place(low, c, 0)

        @pl.when(me < n - 1)
        def _():
            halo(c, 1).wait_recv()
            place(high, c, 2 * rows)

    chunk = epochs * 3 * rows

    def stack(k, v):
        sums = [None] * cells
        for e in range(epochs):
            start = LANES + col_ref[e, v]
            skip = start // LANES
            shift = start - skip * LANES
            turn = lax.rem(LANES - shift, LANES)
            base = skip * chunk + e * 3 * rows + rows + row_ref[e, v]
            keep = lane[:rows] < LANES - shift
            turned = [
                pltpu.roll(
                    field[pl.ds(base + (k * (cells + 2) + c) * chunk, rows), :], turn, 1
                )
                for c in range(cells + 1)
            ]
            for c in range(cells):
                piece = jnp.where(keep, turned[c], turned[c + 1])
                sums[c] = piece if e == 0 else sums[c] + piece
        return sums

    def psi_at(v, c):
        return pl.ds(pl.multiple_of((v * cells + c) * rows, rows), rows)

    def psi_stack(v, carry):
        for c, total in enumerate(stack(0, v)):
            psi_sums[psi_at(v, c), :] = total
        return carry

    def phi_stack(v, best):
        sums = stack(1, v)
        return tuple(
            jnp.maximum(
                best[c], psi_sums[psi_at(v, c), :] / jnp.sqrt(jnp.maximum(sums[c], 1.0))
            )
            for c in range(cells)
        )

    for c in range(chunks):
        all_data(c).wait_recv()
        sum_chunk(c)
        start_halo(c)
    finish_halo(0)
    lax.fori_loop(0, vels, psi_stack, 0, unroll=UNROLL)
    for c in range(1, chunks):
        finish_halo(c)

    best = lax.fori_loop(
        0,
        vels,
        phi_stack,
        (jnp.full((rows, LANES), -jnp.inf, jnp.float32),) * cells,
        unroll=UNROLL,
    )
    for c in range(cells):
        out_ref[:, pl.ds(c * LANES, LANES)] = best[c]

    all_codes().wait_send()
    for c in range(chunks):
        all_data(c).wait_send()

    @pl.when(me < n - 1)
    def _():
        for c in range(chunks):
            halo(c, 0).wait_send()

    @pl.when(me > 0)
    def _():
        for c in range(chunks):
            halo(c, 1).wait_send()


def body(psi, phi, dest_tile, dest_cell, kernel_id, weight, kernels, row_offsets, col_offsets):
    n = lax.axis_size("tile")
    cells, epochs, rows, width = psi.shape
    items = cells * epochs
    cap = max(2, 2 * items // n)
    slots = n * cap
    vels = row_offsets.shape[1]
    code_lanes = -(-slots // LANES) * LANES
    pitch = 2 * rows
    f32 = jnp.float32
    return pl.pallas_call(
        functools.partial(
            kernel, (n, cap, cells, epochs, rows, kernels.shape[0], vels)
        ),
        out_shape=pltpu.VMEM((rows, cells * width), f32),
        in_specs=[pl.BlockSpec(memory_space=pl.ANY)] * 9,
        out_specs=pl.BlockSpec(memory_space=pltpu.VMEM),
        scratch_shapes=[
            pltpu.VMEM(psi.shape, f32),
            pltpu.VMEM(phi.shape, f32),
            pltpu.SMEM((cells, epochs), jnp.int32),
            pltpu.SMEM((cells, epochs), jnp.int32),
            pltpu.SMEM((cells, epochs), jnp.int32),
            pltpu.SMEM((cells, epochs), f32),
            pltpu.VMEM(kernels.shape, f32),
            pltpu.SMEM(row_offsets.shape, jnp.int32),
            pltpu.SMEM(col_offsets.shape, jnp.int32),
            pltpu.VMEM((vels * cells * rows, width), f32),
            pltpu.VMEM((3 * kernels.shape[0], width), f32),
            pltpu.VMEM((items * pitch, width), f32),
            pltpu.VMEM((slots * pitch, width), f32),
            pltpu.VMEM((slots * pitch, width), f32),
            pltpu.VMEM((n, 1, code_lanes), f32),
            pltpu.VMEM((n, 1, code_lanes), f32),
            pltpu.VMEM((items * pitch, width), f32),
            pltpu.VMEM((items * pitch, width), f32),
            pltpu.VMEM((items * pitch, width), f32),
            pltpu.VMEM((2 * (cells + 2) * epochs * 3 * rows, width), f32),
            pltpu.SemaphoreType.DMA((9,)),
            pltpu.SemaphoreType.DMA((3,)),
            pltpu.SemaphoreType.DMA((3,)),
            pltpu.SemaphoreType.DMA,
            pltpu.SemaphoreType.DMA,
            pltpu.SemaphoreType.DMA((2, 3)),
            pltpu.SemaphoreType.DMA((2, 3)),
            pltpu.SemaphoreType.REGULAR,
        ],
        compiler_params=pltpu.CompilerParams(collective_id=0, has_side_effects=True),
    )(
        psi,
        phi,
        dest_tile.reshape(cells, epochs),
        dest_cell,
        kernel_id,
        weight,
        kernels,
        row_offsets,
        col_offsets,
    )


def solution(mesh):
    placed = (
        P(("field", "tile"), None, None, None),
        P(("field", "tile"), None, None, None),
        P(("field", "tile"), None, None),
        P(("field", "tile"), None),
        P(("field", "tile"), None),
        P(("field", "tile"), None),
        P(),
        P("field", None),
        P("field", None),
    )
    return jax.shard_map(
        body, mesh=mesh, in_specs=placed, out_specs=P(("field", "tile"), None), check_vma=False
    )
```

```python
import functools

import jax
import jax.numpy as jnp
from jax import lax
from jax.experimental import pallas as pl
from jax.experimental.pallas import tpu as pltpu
from jax.sharding import PartitionSpec as P

MESH = pl.DeviceIdType.MESH
LANES = 128
UNROLL = 4


def split2(x):
    hi = x.astype(jnp.bfloat16)
    return hi, (x - hi.astype(jnp.float32)).astype(jnp.bfloat16)


def select_dot(onehot2, x):
    return jnp.dot(
        onehot2, jnp.concatenate(split2(x), axis=0), preferred_element_type=jnp.float32
    )


def kernel(
    dims,
    psi_hbm,
    phi_hbm,
    tile_hbm,
    cell_hbm,
    kid_hbm,
    weight_hbm,
    kern_hbm,
    row_hbm,
    col_hbm,
    out_ref,
    psi_ref,
    phi_ref,
    tile_ref,
    cell_ref,
    kid_ref,
    weight_ref,
    kern_ref,
    row_ref,
    col_ref,
    psi_sums,
    taps,
    moved,
    send,
    recv,
    codes_out,
    codes_in,
    own,
    low,
    high,
    field,
    in_sem,
    send_sem,
    recv_sem,
    code_send_sem,
    code_recv_sem,
    halo_send_sem,
    halo_recv_sem,
    near_sem,
    shifts,
):
    n, cap, cells, epochs, rows, kernels, vels = dims
    items = cells * epochs
    slots = n * cap
    pitch = 2 * rows
    parts = (rows, rows)
    firsts = (0, rows)
    chunks = len(parts)
    targets = cells * epochs
    code_lanes = codes_in.shape[2]
    me = lax.axis_index("tile")
    half = n // 2
    side = me // half

    def across(act):
        def step_of(step, carry):
            act((1 - side) * half + lax.rem(me + step, half))
            return carry

        lax.fori_loop(0, half, step_of, 0, unroll=8)

    def beside(act):
        def step_of(step, carry):
            act(side * half + lax.rem(me + step, half))
            return carry

        lax.fori_loop(1, half, step_of, 0, unroll=7)

    def around(act):
        def step_of(step, carry):
            act(lax.rem(me + step, n))
            return carry

        lax.fori_loop(1, n, step_of, 0, unroll=5)

    barrier = pltpu.get_barrier_semaphore()
    around(
        lambda peer: pl.semaphore_signal(
            barrier, inc=1, device_id={"tile": peer}, device_id_type=MESH
        )
    )

    sources = (tile_hbm, cell_hbm, kid_hbm, weight_hbm, kern_hbm, psi_hbm, phi_hbm, row_hbm, col_hbm)
    places = (tile_ref, cell_ref, kid_ref, weight_ref, kern_ref, psi_ref, phi_ref, row_ref, col_ref)
    loads = [
        pltpu.make_async_copy(source, place, in_sem.at[i])
        for i, (source, place) in enumerate(zip(sources, places))
    ]
    for load in loads:
        load.start()
    field[...] = jnp.zeros_like(field)

    lane = lax.broadcasted_iota(jnp.int32, (8, LANES), 1)
    sub = lax.broadcasted_iota(jnp.int32, (8, LANES), 0)
    loads[4].wait()
    for k in range(kernels):
        sums = [jnp.zeros((8, LANES), jnp.float32)] * 3
        for group in range(LANES // 8):
            rows_of = kern_ref[k, pl.ds(group * 8, 8), :]
            gap = lane - sub - group * 8
            sums = [
                jnp.where(gap == off, rows_of, total) for off, total in zip((1, 0, -1), sums)
            ]
        for tap in range(3):
            taps[pl.ds(tap * kernels + k, 1), :] = jnp.sum(sums[tap], axis=0, keepdims=True)

    for load in loads[:4]:
        load.wait()
    row_tile = jnp.full((8, LANES), -1, jnp.int32)
    row_code = jnp.zeros((8, LANES), jnp.int32)
    col_tile = [jnp.full((8, LANES), -1, jnp.int32) for _ in range(items // 8)]
    for b in range(cells):
        for e in range(epochs):
            i = b * epochs + e
            tile = tile_ref[b, e]
            row_tile = jnp.where(lane == i, tile, row_tile)
            row_code = jnp.where(lane == i, cell_ref[b, e] * epochs + e + 1, row_code)
            col_tile[i // 8] = jnp.where(sub == i % 8, tile, col_tile[i // 8])

    def move(k, ref):
        for b in range(cells):
            for e in range(epochs):
                i = b * epochs + e
                kid = kid_ref[b, e]
                weight = weight_ref[b, e]
                before = taps[pl.ds(kid, 1), :] * weight
                centre = taps[pl.ds(kernels + kid, 1), :] * weight
                after = taps[pl.ds(2 * kernels + kid, 1), :] * weight
                x = ref[b, e]
                moved[pl.ds(i * pitch + k * rows, rows), :] = (
                    pltpu.roll(x, 1, 1) * before
                    + x * centre
                    + pltpu.roll(x, LANES - 1, 1) * after
                )

    col_tile = jnp.concatenate(col_tile, axis=0)
    item_lane = lax.broadcasted_iota(jnp.int32, (items, LANES), 1)
    item_sub = lax.broadcasted_iota(jnp.int32, (items, LANES), 0)
    same = (col_tile == row_tile[0:1, :]).astype(jnp.float32)
    row_rank = jnp.sum(jnp.where(item_sub < item_lane, same, 0.0), axis=0, keepdims=True)
    col_rank = jnp.sum(jnp.where(item_lane < item_sub, same, 0.0), axis=1, keepdims=True)
    row_place = jnp.where(
        row_tile[0:1, :] >= 0, row_tile[0:1, :] * cap + row_rank.astype(jnp.int32), -1
    )
    pick = (
        lax.broadcasted_iota(jnp.int32, (slots, LANES), 0) == row_place
    ).astype(jnp.float32)[:, :items]
    pick2 = jnp.concatenate([pick] * 2, axis=1).astype(jnp.bfloat16)

    def block(c, t):
        span = cap * parts[c]
        return pl.ds(pl.multiple_of(slots * firsts[c] + t * span, span), span)

    def pack(c):
        for q in range(0, parts[c], 2):
            x = jnp.concatenate(
                [
                    moved[pl.ds(firsts[c] + q + h, items, stride=pitch), :]
                    for h in range(2)
                ],
                axis=1,
            )
            packed = select_dot(pick2, x)
            for h in range(2):
                send[pl.ds(slots * firsts[c] + q + h, slots, stride=parts[c]), :] = packed[
                    :, h * LANES : (h + 1) * LANES
                ]
        recv[block(c, me), :] = send[block(c, me), :]

    loads[5].wait()
    move(0, psi_ref)
    pack(0)
    named = jnp.where(
        lax.broadcasted_iota(jnp.int32, (n, LANES), 0) == row_tile[0:1, :],
        row_code[0:1, :].astype(jnp.float32),
        0.0,
    )[:, :items].astype(jnp.bfloat16)
    spread = (
        lax.broadcasted_iota(jnp.int32, (items, code_lanes), 1)
        == me * cap + col_rank.astype(jnp.int32)
    ).astype(jnp.bfloat16)
    codes = jnp.dot(named, spread, preferred_element_type=jnp.float32)
    for t in range(n):
        codes_out[t] = codes[t : t + 1, :]

    codes_in[me] = codes_out[me]

    def code_copy(peer):
        return pltpu.make_async_remote_copy(
            src_ref=codes_out.at[peer],
            dst_ref=codes_in.at[me],
            send_sem=code_send_sem,
            recv_sem=code_recv_sem,
            device_id={"tile": peer},
            device_id_type=MESH,
        )

    def all_codes():
        return pltpu.make_async_remote_copy(
            src_ref=codes_out.at[pl.ds(0, n - 1)],
            dst_ref=codes_in.at[pl.ds(0, n - 1)],
            send_sem=code_send_sem,
            recv_sem=code_recv_sem,
            device_id={"tile": lax.rem(me + 1, n)},
            device_id_type=MESH,
        )

    def data_copy(c, peer):
        return pltpu.make_async_remote_copy(
            src_ref=send.at[block(c, peer)],
            dst_ref=recv.at[block(c, me)],
            send_sem=send_sem.at[c],
            recv_sem=recv_sem.at[c],
            device_id={"tile": peer},
            device_id_type=MESH,
        )

    def all_data(c):
        rest = pl.ds(slots * firsts[c], (n - 1) * cap * parts[c])
        return pltpu.make_async_remote_copy(
            src_ref=send.at[rest],
            dst_ref=recv.at[rest],
            send_sem=send_sem.at[c],
            recv_sem=recv_sem.at[c],
            device_id={"tile": lax.rem(me + 1, n)},
            device_id_type=MESH,
        )

    def start_codes(peer):
        code_copy(peer).start()

    def start_data(c):
        return lambda peer: data_copy(c, peer).start()

    pl.semaphore_wait(barrier, n - 1)
    around(start_codes)
    around(start_data(0))
    loads[6].wait()
    move(1, phi_ref)
    for c in range(1, chunks):
        pack(c)
        around(start_data(c))
    for load in loads[7:]:
        load.wait()
    chunk = epochs * 3 * rows

    def plan(v, carry):
        for e in range(epochs):
            start = LANES + col_ref[e, v]
            shift = start & (LANES - 1)
            skip = lax.shift_right_logical(start, LANES.bit_length() - 1)
            shifts[v, e] = skip * chunk + e * 3 * rows + rows + row_ref[e, v]
            shifts[v, epochs + e] = (LANES - shift) & (LANES - 1)
            shifts[v, 2 * epochs + e] = LANES - shift
        return carry

    lax.fori_loop(0, vels, plan, 0)

    all_codes().wait_recv()
    code_row = codes_in[0]
    for t in range(1, n):
        code_row = code_row + codes_in[t]
    land = (
        lax.broadcasted_iota(jnp.int32, (targets, code_lanes), 0) + 1
        == code_row.astype(jnp.int32)
    ).astype(jnp.float32)[:, :slots]
    land2 = jnp.concatenate([land] * 2, axis=1).astype(jnp.bfloat16)

    def share(c):
        return pl.ds(targets * firsts[c], targets * parts[c])

    def halo(c, way):
        peer = (lax.rem(me + 1, n), lax.rem(me + n - 1, n))[way]
        return pltpu.make_async_remote_copy(
            src_ref=own.at[share(c)],
            dst_ref=(low, high)[way].at[share(c)],
            send_sem=halo_send_sem.at[way, c],
            recv_sem=halo_recv_sem.at[way, c],
            device_id={"tile": peer},
            device_id_type=MESH,
        )

    def start_halo(c):
        @pl.when(me < n - 1)
        def _():
            halo(c, 0).start()

        @pl.when(me > 0)
        def _():
            halo(c, 1).start()

    def row_at(k, target):
        return ((k * (cells + 2) + 1) * epochs + target) * 3 * rows

    def sum_chunk(c):
        part = parts[c]
        for q in range(0, part, 2):
            x = jnp.concatenate(
                [
                    recv[pl.ds(slots * firsts[c] + q + h, slots, stride=part), :]
                    for h in range(2)
                ],
                axis=1,
            )
            summed = select_dot(land2, x)
            for h in range(2):
                k, r = divmod(firsts[c] + q + h, rows)
                piece = summed[:, h * LANES : (h + 1) * LANES]
                own[pl.ds(targets * firsts[c] + q + h, targets, stride=part), :] = piece
                field[pl.ds(row_at(k, 0) + rows + r, targets, stride=3 * rows), :] = piece

    def place(ref, c, offset):
        part = parts[c]
        k, r = divmod(firsts[c], rows)
        for target in range(targets):
            field[pl.ds(row_at(k, target) + offset + r, part), :] = ref[
                pl.ds(targets * firsts[c] + target * part, part), :
            ]

    def finish_halo(c):
        @pl.when(me > 0)
        def _():
            halo(c, 0).wait_recv()
            place(low, c, 0)

        @pl.when(me < n - 1)
        def _():
            halo(c, 1).wait_recv()
            place(high, c, 2 * rows)

    def stack(k, v):
        sums = [None] * cells
        for e in range(epochs):
            base = shifts[v, e]
            turn = shifts[v, epochs + e]
            keep = lane[:rows] < shifts[v, 2 * epochs + e]
            turned = [
                pltpu.roll(
                    field[pl.ds(base + (k * (cells + 2) + c) * chunk, rows), :], turn, 1
                )
                for c in range(cells + 1)
            ]
            for c in range(cells):
                piece = jnp.where(keep, turned[c], turned[c + 1])
                sums[c] = piece if e == 0 else sums[c] + piece
        return sums

    def psi_at(v, c):
        return pl.ds(pl.multiple_of((v * cells + c) * rows, rows), rows)

    def psi_stack(v, carry):
        for c, total in enumerate(stack(0, v)):
            psi_sums[psi_at(v, c), :] = total
        return carry

    def phi_stack(v, best):
        sums = stack(1, v)
        return tuple(
            jnp.maximum(
                best[c], psi_sums[psi_at(v, c), :] / jnp.sqrt(jnp.maximum(sums[c], 1.0))
            )
            for c in range(cells)
        )

    for c in range(chunks):
        all_data(c).wait_recv()
        sum_chunk(c)
        start_halo(c)
    finish_halo(0)
    lax.fori_loop(0, vels, psi_stack, 0, unroll=UNROLL)
    for c in range(1, chunks):
        finish_halo(c)

    best = lax.fori_loop(
        0,
        vels,
        phi_stack,
        (jnp.full((rows, LANES), -jnp.inf, jnp.float32),) * cells,
        unroll=UNROLL,
    )
    for c in range(cells):
        out_ref[:, pl.ds(c * LANES, LANES)] = best[c]

    all_codes().wait_send()
    for c in range(chunks):
        all_data(c).wait_send()

    @pl.when(me < n - 1)
    def _():
        for c in range(chunks):
            halo(c, 0).wait_send()

    @pl.when(me > 0)
    def _():
        for c in range(chunks):
            halo(c, 1).wait_send()


def body(psi, phi, dest_tile, dest_cell, kernel_id, weight, kernels, row_offsets, col_offsets):
    n = lax.axis_size("tile")
    cells, epochs, rows, width = psi.shape
    items = cells * epochs
    cap = max(2, 2 * items // n)
    slots = n * cap
    vels = row_offsets.shape[1]
    code_lanes = -(-slots // LANES) * LANES
    pitch = 2 * rows
    f32 = jnp.float32
    return pl.pallas_call(
        functools.partial(
            kernel, (n, cap, cells, epochs, rows, kernels.shape[0], vels)
        ),
        out_shape=pltpu.VMEM((rows, cells * width), f32),
        in_specs=[pl.BlockSpec(memory_space=pl.ANY)] * 9,
        out_specs=pl.BlockSpec(memory_space=pltpu.VMEM),
        scratch_shapes=[
            pltpu.VMEM(psi.shape, f32),
            pltpu.VMEM(phi.shape, f32),
            pltpu.SMEM((cells, epochs), jnp.int32),
            pltpu.SMEM((cells, epochs), jnp.int32),
            pltpu.SMEM((cells, epochs), jnp.int32),
            pltpu.SMEM((cells, epochs), f32),
            pltpu.VMEM(kernels.shape, f32),
            pltpu.SMEM(row_offsets.shape, jnp.int32),
            pltpu.SMEM(col_offsets.shape, jnp.int32),
            pltpu.VMEM((vels * cells * rows, width), f32),
            pltpu.VMEM((3 * kernels.shape[0], width), f32),
            pltpu.VMEM((items * pitch, width), f32),
            pltpu.VMEM((slots * pitch, width), f32),
            pltpu.VMEM((slots * pitch, width), f32),
            pltpu.VMEM((n, 1, code_lanes), f32),
            pltpu.VMEM((n, 1, code_lanes), f32),
            pltpu.VMEM((items * pitch, width), f32),
            pltpu.VMEM((items * pitch, width), f32),
            pltpu.VMEM((items * pitch, width), f32),
            pltpu.VMEM((2 * (cells + 2) * epochs * 3 * rows, width), f32),
            pltpu.SemaphoreType.DMA((9,)),
            pltpu.SemaphoreType.DMA((3,)),
            pltpu.SemaphoreType.DMA((3,)),
            pltpu.SemaphoreType.DMA,
            pltpu.SemaphoreType.DMA,
            pltpu.SemaphoreType.DMA((2, 3)),
            pltpu.SemaphoreType.DMA((2, 3)),
            pltpu.SemaphoreType.REGULAR,
            pltpu.SMEM((vels, 3 * epochs), jnp.int32),
        ],
        compiler_params=pltpu.CompilerParams(collective_id=0, has_side_effects=True),
    )(
        psi,
        phi,
        dest_tile.reshape(cells, epochs),
        dest_cell,
        kernel_id,
        weight,
        kernels,
        row_offsets,
        col_offsets,
    )


def solution(mesh):
    placed = (
        P(("field", "tile"), None, None, None),
        P(("field", "tile"), None, None, None),
        P(("field", "tile"), None, None),
        P(("field", "tile"), None),
        P(("field", "tile"), None),
        P(("field", "tile"), None),
        P(),
        P("field", None),
        P("field", None),
    )
    return jax.shard_map(
        body, mesh=mesh, in_specs=placed, out_specs=P(("field", "tile"), None), check_vma=False
    )
```

```python
import functools

import jax
import jax.numpy as jnp
from jax import lax
from jax.experimental import pallas as pl
from jax.experimental.pallas import tpu as pltpu
from jax.sharding import PartitionSpec as P

MESH = pl.DeviceIdType.MESH
LANES = 128
UNROLL = 8


def split2(x):
    hi = x.astype(jnp.bfloat16)
    return hi, (x - hi.astype(jnp.float32)).astype(jnp.bfloat16)


def select_dot(onehot2, x):
    return jnp.dot(
        onehot2, jnp.concatenate(split2(x), axis=0), preferred_element_type=jnp.float32
    )


def kernel(
    dims,
    psi_hbm,
    phi_hbm,
    tile_hbm,
    cell_hbm,
    kid_hbm,
    weight_hbm,
    kern_hbm,
    row_hbm,
    col_hbm,
    out_ref,
    psi_ref,
    phi_ref,
    tile_ref,
    cell_ref,
    kid_ref,
    weight_ref,
    kern_ref,
    row_ref,
    col_ref,
    scales,
    taps,
    moved,
    send,
    recv,
    codes_out,
    codes_in,
    own,
    low,
    high,
    field,
    in_sem,
    send_sem,
    recv_sem,
    code_send_sem,
    code_recv_sem,
    halo_send_sem,
    halo_recv_sem,
    near_sem,
    shifts,
):
    n, cap, cells, epochs, rows, kernels, vels = dims
    items = cells * epochs
    slots = n * cap
    pitch = 2 * rows
    parts = (rows, rows)
    firsts = (0, rows)
    chunks = len(parts)
    targets = cells * epochs
    code_lanes = codes_in.shape[2]
    me = lax.axis_index("tile")
    half = n // 2
    side = me // half

    def across(act):
        def step_of(step, carry):
            act((1 - side) * half + lax.rem(me + step, half))
            return carry

        lax.fori_loop(0, half, step_of, 0, unroll=8)

    def beside(act):
        def step_of(step, carry):
            act(side * half + lax.rem(me + step, half))
            return carry

        lax.fori_loop(1, half, step_of, 0, unroll=7)

    def around(act):
        def step_of(step, carry):
            act(lax.rem(me + step, n))
            return carry

        lax.fori_loop(1, n, step_of, 0, unroll=5)

    barrier = pltpu.get_barrier_semaphore()
    around(
        lambda peer: pl.semaphore_signal(
            barrier, inc=1, device_id={"tile": peer}, device_id_type=MESH
        )
    )

    sources = (tile_hbm, cell_hbm, kid_hbm, weight_hbm, kern_hbm, phi_hbm, psi_hbm, row_hbm, col_hbm)
    places = (tile_ref, cell_ref, kid_ref, weight_ref, kern_ref, phi_ref, psi_ref, row_ref, col_ref)
    loads = [
        pltpu.make_async_copy(source, place, in_sem.at[i])
        for i, (source, place) in enumerate(zip(sources, places))
    ]
    for load in loads:
        load.start()
    field[...] = jnp.zeros_like(field)

    lane = lax.broadcasted_iota(jnp.int32, (8, LANES), 1)
    sub = lax.broadcasted_iota(jnp.int32, (8, LANES), 0)
    loads[4].wait()
    for k in range(kernels):
        sums = [jnp.zeros((8, LANES), jnp.float32)] * 3
        for group in range(LANES // 8):
            rows_of = kern_ref[k, pl.ds(group * 8, 8), :]
            gap = lane - sub - group * 8
            sums = [
                jnp.where(gap == off, rows_of, total) for off, total in zip((1, 0, -1), sums)
            ]
        for tap in range(3):
            taps[pl.ds(tap * kernels + k, 1), :] = jnp.sum(sums[tap], axis=0, keepdims=True)

    for load in loads[:4]:
        load.wait()
    row_tile = jnp.full((8, LANES), -1, jnp.int32)
    row_code = jnp.zeros((8, LANES), jnp.int32)
    col_tile = [jnp.full((8, LANES), -1, jnp.int32) for _ in range(items // 8)]
    for b in range(cells):
        for e in range(epochs):
            i = b * epochs + e
            tile = tile_ref[b, e]
            row_tile = jnp.where(lane == i, tile, row_tile)
            row_code = jnp.where(lane == i, cell_ref[b, e] * epochs + e + 1, row_code)
            col_tile[i // 8] = jnp.where(sub == i % 8, tile, col_tile[i // 8])

    def move(k, ref):
        for b in range(cells):
            for e in range(epochs):
                i = b * epochs + e
                kid = kid_ref[b, e]
                weight = weight_ref[b, e]
                before = taps[pl.ds(kid, 1), :] * weight
                centre = taps[pl.ds(kernels + kid, 1), :] * weight
                after = taps[pl.ds(2 * kernels + kid, 1), :] * weight
                x = ref[b, e]
                moved[pl.ds(i * pitch + k * rows, rows), :] = (
                    pltpu.roll(x, 1, 1) * before
                    + x * centre
                    + pltpu.roll(x, LANES - 1, 1) * after
                )

    col_tile = jnp.concatenate(col_tile, axis=0)
    item_lane = lax.broadcasted_iota(jnp.int32, (items, LANES), 1)
    item_sub = lax.broadcasted_iota(jnp.int32, (items, LANES), 0)
    same = (col_tile == row_tile[0:1, :]).astype(jnp.float32)
    row_rank = jnp.sum(jnp.where(item_sub < item_lane, same, 0.0), axis=0, keepdims=True)
    col_rank = jnp.sum(jnp.where(item_lane < item_sub, same, 0.0), axis=1, keepdims=True)
    row_place = jnp.where(
        row_tile[0:1, :] >= 0, row_tile[0:1, :] * cap + row_rank.astype(jnp.int32), -1
    )
    pick = (
        lax.broadcasted_iota(jnp.int32, (slots, LANES), 0) == row_place
    ).astype(jnp.float32)[:, :items]
    pick2 = jnp.concatenate([pick] * 2, axis=1).astype(jnp.bfloat16)

    def block(c, t):
        span = cap * parts[c]
        return pl.ds(pl.multiple_of(slots * firsts[c] + t * span, span), span)

    def pack(c):
        for q in range(0, parts[c], 2):
            x = jnp.concatenate(
                [
                    moved[pl.ds(firsts[c] + q + h, items, stride=pitch), :]
                    for h in range(2)
                ],
                axis=1,
            )
            packed = select_dot(pick2, x)
            for h in range(2):
                send[pl.ds(slots * firsts[c] + q + h, slots, stride=parts[c]), :] = packed[
                    :, h * LANES : (h + 1) * LANES
                ]
        recv[block(c, me), :] = send[block(c, me), :]

    loads[5].wait()
    move(0, phi_ref)
    pack(0)
    named = jnp.where(
        lax.broadcasted_iota(jnp.int32, (n, LANES), 0) == row_tile[0:1, :],
        row_code[0:1, :].astype(jnp.float32),
        0.0,
    )[:, :items].astype(jnp.bfloat16)
    spread = (
        lax.broadcasted_iota(jnp.int32, (items, code_lanes), 1)
        == me * cap + col_rank.astype(jnp.int32)
    ).astype(jnp.bfloat16)
    codes = jnp.dot(named, spread, preferred_element_type=jnp.float32)
    for t in range(n):
        codes_out[t] = codes[t : t + 1, :]

    codes_in[me] = codes_out[me]

    def code_copy(peer):
        return pltpu.make_async_remote_copy(
            src_ref=codes_out.at[peer],
            dst_ref=codes_in.at[me],
            send_sem=code_send_sem,
            recv_sem=code_recv_sem,
            device_id={"tile": peer},
            device_id_type=MESH,
        )

    def all_codes():
        return pltpu.make_async_remote_copy(
            src_ref=codes_out.at[pl.ds(0, n - 1)],
            dst_ref=codes_in.at[pl.ds(0, n - 1)],
            send_sem=code_send_sem,
            recv_sem=code_recv_sem,
            device_id={"tile": lax.rem(me + 1, n)},
            device_id_type=MESH,
        )

    def data_copy(c, peer):
        return pltpu.make_async_remote_copy(
            src_ref=send.at[block(c, peer)],
            dst_ref=recv.at[block(c, me)],
            send_sem=send_sem.at[c],
            recv_sem=recv_sem.at[c],
            device_id={"tile": peer},
            device_id_type=MESH,
        )

    def all_data(c):
        rest = pl.ds(slots * firsts[c], (n - 1) * cap * parts[c])
        return pltpu.make_async_remote_copy(
            src_ref=send.at[rest],
            dst_ref=recv.at[rest],
            send_sem=send_sem.at[c],
            recv_sem=recv_sem.at[c],
            device_id={"tile": lax.rem(me + 1, n)},
            device_id_type=MESH,
        )

    def start_codes(peer):
        code_copy(peer).start()

    def start_data(c):
        return lambda peer: data_copy(c, peer).start()

    pl.semaphore_wait(barrier, n - 1)
    around(start_codes)
    around(start_data(0))
    loads[6].wait()
    move(1, psi_ref)
    for c in range(1, chunks):
        pack(c)
        around(start_data(c))
    for load in loads[7:]:
        load.wait()
    chunk = epochs * 3 * rows

    def plan(v, carry):
        for e in range(epochs):
            start = LANES + col_ref[e, v]
            shift = start & (LANES - 1)
            skip = lax.shift_right_logical(start, LANES.bit_length() - 1)
            shifts[v, e] = skip * chunk + e * 3 * rows + rows + row_ref[e, v]
            shifts[v, epochs + e] = (LANES - shift) & (LANES - 1)
            shifts[v, 2 * epochs + e] = LANES - shift
        return carry

    lax.fori_loop(0, vels, plan, 0)

    all_codes().wait_recv()
    code_row = codes_in[0]
    for t in range(1, n):
        code_row = code_row + codes_in[t]
    land = (
        lax.broadcasted_iota(jnp.int32, (targets, code_lanes), 0) + 1
        == code_row.astype(jnp.int32)
    ).astype(jnp.float32)[:, :slots]
    land2 = jnp.concatenate([land] * 2, axis=1).astype(jnp.bfloat16)

    def share(c):
        return pl.ds(targets * firsts[c], targets * parts[c])

    def halo(c, way):
        peer = (lax.rem(me + 1, n), lax.rem(me + n - 1, n))[way]
        return pltpu.make_async_remote_copy(
            src_ref=own.at[share(c)],
            dst_ref=(low, high)[way].at[share(c)],
            send_sem=halo_send_sem.at[way, c],
            recv_sem=halo_recv_sem.at[way, c],
            device_id={"tile": peer},
            device_id_type=MESH,
        )

    def start_halo(c):
        @pl.when(me < n - 1)
        def _():
            halo(c, 0).start()

        @pl.when(me > 0)
        def _():
            halo(c, 1).start()

    def row_at(k, target):
        return ((k * (cells + 2) + 1) * epochs + target) * 3 * rows

    def sum_chunk(c):
        part = parts[c]
        for q in range(0, part, 2):
            x = jnp.concatenate(
                [
                    recv[pl.ds(slots * firsts[c] + q + h, slots, stride=part), :]
                    for h in range(2)
                ],
                axis=1,
            )
            summed = select_dot(land2, x)
            for h in range(2):
                k, r = divmod(firsts[c] + q + h, rows)
                piece = summed[:, h * LANES : (h + 1) * LANES]
                own[pl.ds(targets * firsts[c] + q + h, targets, stride=part), :] = piece
                field[pl.ds(row_at(k, 0) + rows + r, targets, stride=3 * rows), :] = piece

    def place(ref, c, offset):
        part = parts[c]
        k, r = divmod(firsts[c], rows)
        for target in range(targets):
            field[pl.ds(row_at(k, target) + offset + r, part), :] = ref[
                pl.ds(targets * firsts[c] + target * part, part), :
            ]

    def finish_halo(c):
        @pl.when(me > 0)
        def _():
            halo(c, 0).wait_recv()
            place(low, c, 0)

        @pl.when(me < n - 1)
        def _():
            halo(c, 1).wait_recv()
            place(high, c, 2 * rows)

    def stack(k, v):
        sums = [None] * cells
        for e in range(epochs):
            base = shifts[v, e]
            turn = shifts[v, epochs + e]
            keep = lane[:rows] < shifts[v, 2 * epochs + e]
            turned = [
                pltpu.roll(
                    field[pl.ds(base + (k * (cells + 2) + c) * chunk, rows), :], turn, 1
                )
                for c in range(cells + 1)
            ]
            for c in range(cells):
                piece = jnp.where(keep, turned[c], turned[c + 1])
                sums[c] = piece if e == 0 else sums[c] + piece
        return sums

    def scale_at(v, c):
        return pl.ds(pl.multiple_of((v * cells + c) * rows, rows), rows)

    def phi_stack(v, carry):
        for c, total in enumerate(stack(0, v)):
            scales[scale_at(v, c), :] = 1.0 / jnp.sqrt(jnp.maximum(total, 1.0))
        return carry

    def psi_stack(v, best):
        sums = stack(1, v)
        return tuple(
            jnp.maximum(best[c], sums[c] * scales[scale_at(v, c), :]) for c in range(cells)
        )

    for c in range(chunks):
        all_data(c).wait_recv()
        sum_chunk(c)
        start_halo(c)
    finish_halo(0)
    lax.fori_loop(0, vels, phi_stack, 0, unroll=UNROLL)
    for c in range(1, chunks):
        finish_halo(c)

    best = lax.fori_loop(
        0,
        vels,
        psi_stack,
        (jnp.full((rows, LANES), -jnp.inf, jnp.float32),) * cells,
        unroll=UNROLL,
    )
    for c in range(cells):
        out_ref[:, pl.ds(c * LANES, LANES)] = best[c]

    all_codes().wait_send()
    for c in range(chunks):
        all_data(c).wait_send()

    @pl.when(me < n - 1)
    def _():
        for c in range(chunks):
            halo(c, 0).wait_send()

    @pl.when(me > 0)
    def _():
        for c in range(chunks):
            halo(c, 1).wait_send()


def body(psi, phi, dest_tile, dest_cell, kernel_id, weight, kernels, row_offsets, col_offsets):
    n = lax.axis_size("tile")
    cells, epochs, rows, width = psi.shape
    items = cells * epochs
    cap = max(2, 2 * items // n)
    slots = n * cap
    vels = row_offsets.shape[1]
    code_lanes = -(-slots // LANES) * LANES
    pitch = 2 * rows
    f32 = jnp.float32
    return pl.pallas_call(
        functools.partial(
            kernel, (n, cap, cells, epochs, rows, kernels.shape[0], vels)
        ),
        out_shape=pltpu.VMEM((rows, cells * width), f32),
        in_specs=[pl.BlockSpec(memory_space=pl.ANY)] * 9,
        out_specs=pl.BlockSpec(memory_space=pltpu.VMEM),
        scratch_shapes=[
            pltpu.VMEM(psi.shape, f32),
            pltpu.VMEM(phi.shape, f32),
            pltpu.SMEM((cells, epochs), jnp.int32),
            pltpu.SMEM((cells, epochs), jnp.int32),
            pltpu.SMEM((cells, epochs), jnp.int32),
            pltpu.SMEM((cells, epochs), f32),
            pltpu.VMEM(kernels.shape, f32),
            pltpu.SMEM(row_offsets.shape, jnp.int32),
            pltpu.SMEM(col_offsets.shape, jnp.int32),
            pltpu.VMEM((vels * cells * rows, width), f32),
            pltpu.VMEM((3 * kernels.shape[0], width), f32),
            pltpu.VMEM((items * pitch, width), f32),
            pltpu.VMEM((slots * pitch, width), f32),
            pltpu.VMEM((slots * pitch, width), f32),
            pltpu.VMEM((n, 1, code_lanes), f32),
            pltpu.VMEM((n, 1, code_lanes), f32),
            pltpu.VMEM((items * pitch, width), f32),
            pltpu.VMEM((items * pitch, width), f32),
            pltpu.VMEM((items * pitch, width), f32),
            pltpu.VMEM((2 * (cells + 2) * epochs * 3 * rows, width), f32),
            pltpu.SemaphoreType.DMA((9,)),
            pltpu.SemaphoreType.DMA((3,)),
            pltpu.SemaphoreType.DMA((3,)),
            pltpu.SemaphoreType.DMA,
            pltpu.SemaphoreType.DMA,
            pltpu.SemaphoreType.DMA((2, 3)),
            pltpu.SemaphoreType.DMA((2, 3)),
            pltpu.SemaphoreType.REGULAR,
            pltpu.SMEM((vels, 3 * epochs), jnp.int32),
        ],
        compiler_params=pltpu.CompilerParams(collective_id=0, has_side_effects=True),
    )(
        psi,
        phi,
        dest_tile.reshape(cells, epochs),
        dest_cell,
        kernel_id,
        weight,
        kernels,
        row_offsets,
        col_offsets,
    )


def solution(mesh):
    placed = (
        P(("field", "tile"), None, None, None),
        P(("field", "tile"), None, None, None),
        P(("field", "tile"), None, None),
        P(("field", "tile"), None),
        P(("field", "tile"), None),
        P(("field", "tile"), None),
        P(),
        P("field", None),
        P("field", None),
    )
    return jax.shard_map(
        body, mesh=mesh, in_specs=placed, out_specs=P(("field", "tile"), None), check_vma=False
    )
```
